32 devices in a mesh: sub: 8 (over z, y), col: 4 (over x, core).
Axes of the slice: x: 2, y: 2, z: 4, core: 2. Of those that a mesh axis runs over, the one named last changes fastest.
Arguments:
- rhs: bfloat16 [32, 1024, 128], P(('sub', 'col')), may hold values from -64 to 64
- schur: bfloat16 [32, 1024, 1024], P(('sub', 'col')), may hold values from -1 to 3
- local_inverse: bfloat16 [32, 1024, 1024], P(('sub', 'col')), may hold values from -1 to 2
- basis: bfloat16 [32, 8, 1024], P(('sub', 'col')), may hold values from -0.75 to 0.75
- coarse_inverse: bfloat16 [256, 256], P('sub', 'col'), may hold values from -1 to 2
- primal_index: int32 [32, 8], P(('sub', 'col')), may hold values from 0 to 255, as said below
- neighbour_dof: int32 [32, 1024], P(('sub', 'col')), may hold values from 0 to 1023, as said below
Outputs:
- solution: bfloat16 [32, 1024, 128], P(('sub', 'col'))
The draws below stay inside these ranges and needn't reach their ends.
Inputs may be any that keep to these rules, and one draw needn't show every extreme that they name: `neighbour_dof`: each subdomain's unknowns in one shared block name places in the neighbour's facing block (for [0, 256) the neighbour's [256, 512), and so on), and the neighbour's entry names the place back. `primal_index`: every coarse unknown is named exactly once over all subdomains.
All inputs are finite; a program needn't handle non-finite values.
Results may differ from the reference program's by a relative error of at most 0.004.
The reference program's roundings to bfloat16 on the way (of `half`, `weighted`, `coarse_load`, `coarse_vector` and `coarse_solution`) count: a program that leaves them out, or rounds other values in their place, can miss the bound.
Values may be sent and summed in bfloat16 or wider, within the bound.
A program may use at most 64 MiB of HBM per device.

```python
import math
import jax
import jax.numpy as jnp
from jax import lax

IFACE = 1024
PRIM = 8
CASES = 128
SUBROWS = 8
SUBCOLS = 4
SUBS = 32
COARSE = 256


def dominant(item_key, order, lowest, highest, spread):
    diag_key, rest_key = jax.random.split(item_key)
    diag_values = jax.random.uniform(diag_key, (order,), jnp.float32, lowest, highest)
    rest = jax.random.normal(rest_key, (order, order), jnp.float32) * (spread / math.sqrt(order))
    return jnp.clip(rest + jnp.diag(diag_values), -1.0, highest)


def draw_rhs(key, part):
    base_key = jax.random.fold_in(key, 0)
    case_key = jax.random.fold_in(key, 2)
    position = jnp.arange(SUBS, dtype=jnp.float32) / max(SUBS - 1, 1)
    values = jax.random.normal(base_key, (SUBS, IFACE, CASES), jnp.float32)
    rising = jnp.exp(jnp.log(3.0) * position)
    case_scale = jnp.exp(jax.random.uniform(case_key, (CASES,), jnp.float32, 0.0, math.log(10.0)))
    return (values * rising[:, None, None] * case_scale / 5.0).astype(jnp.bfloat16)


def draw_schur(key, part):
    keys = jax.random.split(key, SUBS)
    return lax.map(lambda item_key: dominant(item_key, IFACE, 1.5, 3.0, 0.5).astype(jnp.bfloat16), keys)


def draw_local_inverse(key, part):
    keys = jax.random.split(jax.random.fold_in(key, 7), SUBS)
    return lax.map(lambda item_key: dominant(item_key, IFACE, 1.0, 2.0, 0.35).astype(jnp.bfloat16), keys)


def draw_coarse_inverse(key, part):
    return dominant(jax.random.fold_in(key, 11), COARSE, 1.0, 2.0, 0.35).astype(jnp.bfloat16)


def draw_primal_index(key, part):
    return jax.random.permutation(jax.random.fold_in(key, 13), COARSE).reshape(SUBS, PRIM).astype(jnp.int32)


def draw_neighbour_dof(key, part):
    face_size = IFACE // 4
    row_key, side_key = jax.random.split(jax.random.fold_in(key, 17))

    def orders(item_key):
        keys = jax.random.split(item_key, SUBS)
        table = jax.vmap(lambda single_key: jax.random.permutation(single_key, face_size))(keys)
        return table.reshape(SUBROWS, SUBCOLS, face_size)

    def invert(table):
        return jnp.argsort(table, axis=-1, stable=True)
    down_order = orders(row_key)
    side_order = orders(side_key)
    lower_sub = jnp.roll(invert(down_order), 1, axis=0) + face_size
    upper_sub = down_order + 0
    lower_col = jnp.roll(invert(side_order), 1, axis=1) + 3 * face_size
    upper_col = side_order + 2 * face_size
    joined = jnp.concatenate([lower_sub, upper_sub, lower_col, upper_col], axis=-1)
    return joined.reshape(SUBS, IFACE).astype(jnp.int32)


def block_scale(key, dims, shards, least, largest):
    loudness, own = 1.0, jax.random.fold_in(key, 6)
    for dim, blocks in shards:
        heights = jnp.exp(jax.random.uniform(jax.random.fold_in(own, dim), (blocks,), jnp.float32, least / len(shards), largest / len(shards)))
        loudness = loudness * jnp.repeat(heights, dims[dim] // blocks).reshape([-1 if axis == dim else 1 for axis in range(len(dims))])
    return loudness


def centred(key, extent, scale, reach, cuts=(), kind=jnp.bfloat16):
    array = jax.random.normal(key, extent, jnp.float32) * scale
    if len(cuts) > 0:
        array = block_scale(key, extent, cuts, -0.22, 0.18) * array
    return jnp.clip(array, min=-reach, max=reach).astype(kind)


def setup_inputs(seed: int = 0) -> dict:
    seeds = jax.random.split(jax.random.key(seed), 8)
    return {
        "rhs": draw_rhs(jax.random.fold_in(seeds[7], 71), 0),
        "schur": draw_schur(jax.random.fold_in(seeds[7], 71), 0),
        "local_inverse": draw_local_inverse(jax.random.fold_in(seeds[7], 71), 0),
        "basis": centred(seeds[3], (SUBS, PRIM, IFACE), (IFACE // 16) ** -0.5, 0.75, ((0, 32),)),
        "coarse_inverse": draw_coarse_inverse(jax.random.fold_in(seeds[7], 71), 0),
        "primal_index": draw_primal_index(jax.random.fold_in(seeds[7], 71), 0),
        "neighbour_dof": draw_neighbour_dof(jax.random.fold_in(seeds[7], 71), 0),
    }


def half(value):
    return value.astype(jnp.bfloat16)


def assemble(field, neighbour_dof):
    face_size = IFACE // 4
    grid_view = field.reshape(SUBROWS, SUBCOLS, IFACE, CASES)
    link_table = neighbour_dof.reshape(SUBROWS, SUBCOLS, IFACE)
    incoming = [
        jnp.roll(grid_view[:, :, face_size:2 * face_size], 1, axis=0),
        jnp.roll(grid_view[:, :, 0:face_size], -1, axis=0),
        jnp.roll(grid_view[:, :, 3 * face_size:], 1, axis=1),
        jnp.roll(grid_view[:, :, 2 * face_size:3 * face_size], -1, axis=1),
    ]
    offsets = [face_size, 0, 3 * face_size, 2 * face_size]
    picker = jax.vmap(jax.vmap(lambda source, places: source[places]))
    collected = []
    for number in range(4):
        places = link_table[:, :, number * face_size:(number + 1) * face_size] - offsets[number]
        collected.append(picker(incoming[number], places.astype(jnp.int32)))
    return field + jnp.concatenate(collected, axis=2).reshape(SUBS, IFACE, CASES)


def inner(left_field, right_field):
    return 0.5 * jnp.sum(left_field * right_field, axis=(0, 1))


def block_products(matrices, operands):
    def single(paired):
        return jnp.dot(paired[0], paired[1], preferred_element_type=jnp.float32)
    return lax.map(single, (matrices, operands))


def schur_image(direction, schur, neighbour_dof):
    return assemble(block_products(schur, half(direction)), neighbour_dof)


def precondition(residual, local_inverse, basis, coarse_inverse, primal_index, neighbour_dof):
    weighted = half(residual * 0.5)
    local_part = block_products(local_inverse, weighted)
    coarse_load = half(block_products(basis, weighted))
    coarse_vector = jnp.zeros((COARSE, CASES), jnp.bfloat16)
    coarse_vector = coarse_vector.at[primal_index.reshape(-1)].set(coarse_load.reshape(SUBS * PRIM, CASES))
    coarse_solution = half(jnp.dot(coarse_inverse, coarse_vector, preferred_element_type=jnp.float32))
    taken = coarse_solution[primal_index]

    def lift(paired):
        return lax.dot_general(paired[0], paired[1], (((0,), (0,)), ((), ())), preferred_element_type=jnp.float32)

    correction = lax.map(lift, (basis, taken))
    return assemble((local_part + correction) * 0.5, neighbour_dof)


def reference(rhs, schur, local_inverse, basis, coarse_inverse, primal_index, neighbour_dof):
    residual = assemble(rhs.astype(jnp.float32), neighbour_dof)
    first = precondition(residual, local_inverse, basis, coarse_inverse, primal_index, neighbour_dof)
    rz_first = inner(residual, first)
    image = schur_image(first, schur, neighbour_dof)
    alpha = rz_first / inner(first, image)
    return half(alpha * first)
```

```python
import functools
import math

import jax
import jax.numpy as jnp
from jax import lax
from jax.experimental import pallas as pl
from jax.experimental.pallas import tpu as pltpu
from jax.sharding import PartitionSpec as P

MESH = pl.DeviceIdType.MESH
F32 = jnp.float32
BF16 = jnp.bfloat16


def kernel(
    subs, cols,
    rhs_hbm, schur_hbm, inverse_hbm, basis_hbm, coarse_hbm, index_hbm, links_hbm,
    first_ref, alpha_ref,
    basis_ref, index_ref, links_ref, rhs_ref, schur_ref, inverse_ref,
    picks, halo_rhs, halo_z, halo_basis, lift, given, z_ref, z_half, p_half, image_ref,
    indices, slab, picked, chosen, arrived, columns, loads, sums,
    local_sem, halo_send, halo_recv, z_send, z_recv, basis_send, basis_recv, all_send, all_recv,
    face_ack, all_ack,
):
    count = subs * cols
    row = lax.axis_index("sub")
    column = lax.axis_index("col")
    me = row * cols + column
    size = rhs_ref.shape[0]
    face = size // 4
    primals = index_ref.shape[1]
    height, width = coarse_hbm.shape
    cases = rhs_ref.shape[1]
    blocks = 5 * primals
    group = math.gcd(count, 32)
    straight = count <= 64

    def place(target):
        return (target // cols, target % cols)

    def span(f):
        return pl.ds(pl.multiple_of(f * face, face), face)

    half_way = (row * 2) // subs

    def each_other(act):
        def body(step, carry):
            q = step // cols
            high, low = subs - 1 - q, q
            high = high - (row - high + subs) // subs
            low = low + (low - row + subs) // subs
            target_row = (1 - half_way) * high + half_way * low
            act((target_row, (column + step) % cols))
            return carry

        lax.fori_loop(0, (subs - 1) * cols, body, 0, unroll=straight)
        for step in range(1, cols):
            act((row, (column + step) % cols))

    def loop(start, stop, act):
        def body(target, carry):
            act(target)
            return carry

        lax.fori_loop(start, stop, body, 0)

    barrier = pltpu.get_barrier_semaphore()
    loop(
        me + 1, count,
        lambda target: pl.semaphore_signal(
            barrier, inc=1, device_id=place(target), device_id_type=MESH
        ),
    )

    small_loads = [
        pltpu.make_async_copy(source, target, local_sem.at[4 + number])
        for number, (source, target) in enumerate(
            ((links_hbm, links_ref), (index_hbm, index_ref), (basis_hbm, basis_ref),
             (coarse_hbm, slab.at[pl.ds(row * height, height)]))
        )
    ]
    for load in small_loads:
        load.start()
    load_rhs = pltpu.make_async_copy(rhs_hbm.at[0], rhs_ref, local_sem.at[0])
    load_inverse = pltpu.make_async_copy(inverse_hbm.at[0], inverse_ref, local_sem.at[1])
    load_schur = pltpu.make_async_copy(schur_hbm.at[0], schur_ref, local_sem.at[2])
    load_rhs.start()
    load_inverse.start()
    load_schur.start()

    def facing(g):
        return 1 - g if g < 2 else 5 - g

    def partner(g):
        if g < 2:
            return ((row + subs + 2 * g - 1) % subs, column)
        return (row, (column + cols + 2 * g - 5) % cols)

    def exchange(source, target, send, recv, g):
        return pltpu.make_async_remote_copy(
            src_ref=source, dst_ref=target.at[facing(g)], send_sem=send.at[g], recv_sem=recv.at[facing(g)],
            device_id=partner(g), device_id_type=MESH,
        )

    rhs_copies = [
        exchange(rhs_hbm.at[0, pl.ds(g * face, face)], halo_rhs, halo_send, halo_recv, g) for g in range(4)
    ]
    basis_copies = [
        exchange(basis_hbm.at[0, :, pl.ds(g * face, face)], halo_basis, basis_send, basis_recv, g)
        for g in range(4)
    ]
    z_copies = [
        exchange(z_half.at[pl.ds(g * face, face)], halo_z, z_send, z_recv, g) for g in range(4)
    ]

    def row_z_copy(g):
        return pltpu.make_async_remote_copy(
            src_ref=z_half.at[span(g)], dst_ref=halo_z.at[1 - g], send_sem=z_send.at[g], recv_sem=z_recv.at[1 - g],
            device_id=((row + subs + 2 * g - 1) % subs, column), device_id_type=MESH,
        )

    lower = (row > 0, row == subs - 1, column > 0, column == cols - 1)
    higher = (row == 0, row < subs - 1, column == 0, column < cols - 1)

    @pl.when(me > 0)
    def _():
        pl.semaphore_wait(barrier, me)

    for g in (1, 0, 2, 3):
        @pl.when(lower[g])
        def _(g=g):
            pl.semaphore_signal(
                face_ack.at[facing(g)], inc=1, device_id=partner(g), device_id_type=MESH
            )
            rhs_copies[g].start()
            basis_copies[g].start()

    loop(
        0, me,
        lambda target: pl.semaphore_signal(
            all_ack.at[0], inc=1, device_id=place(target), device_id_type=MESH
        ),
    )

    def send_coarse(target):
        pltpu.make_async_remote_copy(
            src_ref=coarse_hbm,
            dst_ref=slab.at[pl.ds(row * height, height)],
            send_sem=all_send.at[4],
            recv_sem=all_recv.at[4],
            device_id=(target, column),
            device_id_type=MESH,
        ).start()

    def send_slot(slots, number):
        return lambda target: pltpu.make_async_remote_copy(
            src_ref=slots.at[me],
            dst_ref=slots.at[me],
            send_sem=all_send.at[number],
            recv_sem=all_recv.at[number],
            device_id=target,
            device_id_type=MESH,
        ).start()

    loop(0, row, send_coarse)
    for load in small_loads:
        load.wait()
    lanes = indices.shape[2]
    indices[me] = jnp.zeros((1, lanes), F32)
    indices[me, :, pl.ds(0, primals)] = index_ref[...].astype(F32)
    loop(0, me, lambda target: send_slot(indices, 0)(place(target)))

    offsets = (face, 0, 3 * face, 2 * face)
    for f in range(4):
        places = links_ref[:, f * face : (f + 1) * face] - offsets[f]
        hit = lax.broadcasted_iota(jnp.int32, (face, face), 0) == places
        picks[f] = jnp.where(hit, 1.0, 0.0).astype(F32).T.astype(BF16)

    for g in (3, 2, 1, 0):
        @pl.when(higher[g])
        def _(g=g):
            pl.semaphore_wait(face_ack.at[g], 1)
            rhs_copies[g].start()
            basis_copies[g].start()

    @pl.when(me < count - 1)
    def _():
        pl.semaphore_wait(all_ack.at[0], count - 1 - me)

    loop(row + 1, subs, send_coarse)
    loop(me + 1, count, lambda target: send_slot(indices, 0)(place(target)))

    def wait_face(target, recv, f):
        pltpu.make_async_copy(target.at[f], target.at[f], recv.at[f]).wait()

    def wait_part(part, sems, number):
        pltpu.make_async_copy(part, part, sems.at[number]).wait()

    others = pl.ds(0, count - 1)

    last = (row + 1) // subs
    load_rhs.wait()
    load = jnp.zeros((primals, cases), F32)
    load_inverse.wait()
    for number, f in enumerate((2, 3, 1 - last, last)):
        block = span(f)
        wait_face(halo_rhs, halo_recv, f)
        got = jnp.dot(picks[f], halo_rhs[f], preferred_element_type=F32)
        residual = rhs_ref[block, :].astype(F32) + got
        first_ref[block, :] = residual
        part = (residual * 0.5).astype(BF16)
        load += jnp.dot(basis_ref[0, :, block], part, preferred_element_type=F32)
        if number == 0:
            for h in range(4):
                rows = span(h)
                z_ref[rows, :] = jnp.dot(inverse_ref[rows, block], part, preferred_element_type=F32)
        elif number < 3:
            for h in range(4):
                rows = span(h)
                z_ref[rows, :] += jnp.dot(inverse_ref[rows, block], part, preferred_element_type=F32)
        else:
            for turn, h in enumerate((last, 1 - last, 2, 3)):
                rows = span(h)
                value = z_ref[rows, :] + jnp.dot(inverse_ref[rows, block], part, preferred_element_type=F32)
                value = value * 0.5
                z_ref[rows, :] = value
                z_half[rows, :] = value.astype(BF16)
                (row_z_copy(h) if turn < 2 else z_copies[h]).start()
                if turn == 0:
                    loads[me] = load.astype(BF16)
                    each_other(send_slot(loads, 1))
    begun = jnp.sum(first_ref[...] * z_ref[...], axis=0, keepdims=True)

    def spread(start, extent, number):
        values = indices[pl.ds(start, number)]
        values = jnp.broadcast_to(values, (number, primals, lanes))
        diagonal = lax.broadcasted_iota(jnp.int32, values.shape, 1) == lax.broadcasted_iota(
            jnp.int32, values.shape, 2
        )
        named = jnp.sum(jnp.where(diagonal, values, 0.0), axis=2, keepdims=True)
        named = named.astype(jnp.int32)
        return jnp.broadcast_to(named, (number, primals, extent))

    wait_part(indices.at[others], all_recv, 0)
    total_rows = subs * height
    chunk = math.gcd(total_rows, 256)
    own = spread(row * cols, chunk, cols)
    up = spread((row + subs - 1) % subs * cols, chunk, cols)
    down = spread((row + 1) % subs * cols, chunk, cols)
    named = jnp.concatenate(
        [
            source[k : k + 1]
            for j in range(cols)
            for source, k in ((own, j), (up, j), (down, j), (own, (j + cols - 1) % cols), (own, (j + 1) % cols))
        ],
        axis=0,
    )
    wait_part(slab.at[pl.ds(0, (subs - 1) * height)], all_recv, 4)

    def choose(k, carry):
        hit = lax.broadcasted_iota(jnp.int32, named.shape, 2) == named - k * chunk
        hit = jnp.where(hit, 1.0, 0.0).astype(F32).reshape(cols * blocks, chunk).astype(BF16)
        part = slab[pl.ds(pl.multiple_of(k * chunk, chunk), chunk), :]
        picked[...] += jnp.dot(hit, part, preferred_element_type=F32)
        return carry

    picked[...] = jnp.zeros_like(picked)
    lax.fori_loop(0, total_rows // chunk, choose, 0)
    chosen[...] = picked[...].reshape(cols, blocks, width).astype(BF16)
    arrived[column] = chosen[column]
    for step in range(1, cols):
        target = (column + step) % cols
        pltpu.make_async_remote_copy(
            src_ref=chosen.at[target],
            dst_ref=arrived.at[column],
            send_sem=all_send.at[3],
            recv_sem=all_recv.at[3],
            device_id=(row, target),
            device_id_type=MESH,
        ).start()

    for f in range(4):
        wait_face(halo_basis, basis_recv, f)
        mine = basis_ref[0, :, f * face : (f + 1) * face].astype(F32) * 0.5
        theirs = halo_basis[f].astype(F32) * 0.5
        both = jnp.concatenate([jnp.zeros_like(theirs), theirs], axis=0).astype(BF16)
        turned = lax.dot_general(picks[f], both, (((1,), (1,)), ((), ())), preferred_element_type=F32)
        kept = jnp.concatenate([mine, jnp.zeros_like(mine)], axis=0).T
        lift[f] = (turned + kept).astype(BF16)

    wait_part(arrived.at[pl.ds(0, cols - 1)], all_recv, 3)

    def arrange(g, carry):
        total = jnp.zeros((blocks, group * primals), F32)
        for j in range(cols):
            named = spread(g * group, width, group) - j * width
            hit = lax.broadcasted_iota(jnp.int32, named.shape, 2) == named
            hit = jnp.where(hit, 1.0, 0.0).astype(F32).reshape(group * primals, width).astype(BF16)
            total += lax.dot_general(
                arrived[j], hit, (((1,), (1,)), ((), ())), preferred_element_type=F32
            )
        columns[g] = total.astype(BF16)
        return carry

    lax.fori_loop(0, count // group, arrange, 0)

    wait_part(loads.at[others], all_recv, 1)

    def solve(g, total):
        part = loads[pl.ds(g * group, group)].astype(F32).reshape(group * primals, cases)
        return total + jnp.dot(columns[g], part.astype(BF16), preferred_element_type=F32)

    taken = lax.fori_loop(0, count // group, solve, jnp.zeros((blocks, cases), F32))
    taken = taken.astype(BF16).astype(F32)
    for f in range(4):
        given[f] = jnp.concatenate(
            [taken[:primals], taken[(f + 1) * primals : (f + 2) * primals]], axis=0
        ).astype(BF16)
    ended = jnp.sum(load * taken[:primals], axis=0, keepdims=True)
    sums[me, pl.ds(0, 1), :] = begun + ended

    load_schur.wait()
    for number, f in enumerate((2, 3, 1 - last, last)):
        block = span(f)
        first = z_ref[block, :] + jnp.dot(lift[f], given[f], preferred_element_type=F32)
        wait_face(halo_z, z_recv, f)
        first = first + jnp.dot(picks[f], halo_z[f], preferred_element_type=F32)
        first_ref[block, :] = first
        part = first.astype(BF16)
        if number == 0:
            for h in range(4):
                rows = span(h)
                image_ref[rows, :] = jnp.dot(schur_ref[rows, block], part, preferred_element_type=F32)
        elif number < 3:
            for h in range(4):
                rows = span(h)
                image_ref[rows, :] += jnp.dot(schur_ref[rows, block], part, preferred_element_type=F32)
        else:
            total = jnp.zeros((1, cases), F32)
            for h in range(4):
                rows = span(h)
                image = image_ref[rows, :] + jnp.dot(
                    schur_ref[rows, block], part, preferred_element_type=F32
                )
                total += jnp.sum(first_ref[rows, :] * image, axis=0, keepdims=True)
    sums[me, pl.ds(1, 1), :] = total
    each_other(send_slot(sums, 2))
    for copy in rhs_copies + basis_copies + z_copies:
        copy.wait_send()
    wait_part(indices.at[others], all_send, 0)
    wait_part(loads.at[others], all_send, 1)
    wait_part(arrived.at[pl.ds(0, cols - 1)], all_send, 3)
    wait_part(slab.at[pl.ds(0, (subs - 1) * height)], all_send, 4)
    wait_part(sums.at[others], all_recv, 2)
    whole = jnp.sum(sums[...], axis=0)
    alpha_ref[...] = whole[0:1, :] / whole[1:2, :]
    wait_part(sums.at[others], all_send, 2)


def solution(mesh):
    subs, cols = mesh.shape["sub"], mesh.shape["col"]
    count = subs * cols

    def step(rhs, schur, local_inverse, basis, coarse_inverse, primal_index, neighbour_dof):
        size, cases = rhs.shape[1:]
        face = size // 4
        primals = primal_index.shape[1]
        height, width = coarse_inverse.shape
        lanes = 128 * pl.cdiv(primals, 128)
        wide = 128 * pl.cdiv(width, 128)
        blocks = 5 * primals
        group = math.gcd(count, 32)
        anywhere = pl.BlockSpec(memory_space=pltpu.HBM)
        near = pl.BlockSpec(memory_space=pltpu.VMEM)
        fixed = 4 * size * size + 8 * face * face + 24 * size * cases + 8 * 128 * size
        slots = count * (4 * 8 * lanes + 2 * primals * cases * 2 + 4 * 8 * cases)
        coarse = 2 * subs * height * wide + 12 * cols * blocks * wide + 4 * count * primals * blocks
        limit = min(fixed + slots + coarse + 6 * 1024 * 1024, 63 * 1024 * 1024)
        first, alpha = pl.pallas_call(
            functools.partial(kernel, subs, cols),
            out_shape=(
                jax.ShapeDtypeStruct((size, cases), F32),
                jax.ShapeDtypeStruct((1, cases), F32),
            ),
            in_specs=[anywhere] * 7,
            out_specs=(near, near),
            scratch_shapes=[
                pltpu.VMEM(basis.shape, BF16),
                pltpu.VMEM(primal_index.shape, jnp.int32),
                pltpu.VMEM(neighbour_dof.shape, jnp.int32),
                pltpu.VMEM((size, cases), BF16),
                pltpu.VMEM((size, size), BF16),
                pltpu.VMEM((size, size), BF16),
                pltpu.VMEM((4, face, face), BF16),
                pltpu.VMEM((4, face, cases), BF16),
                pltpu.VMEM((4, face, cases), BF16),
                pltpu.VMEM((4, primals, face), BF16),
                pltpu.VMEM((4, face, 2 * primals), BF16),
                pltpu.VMEM((4, 2 * primals, cases), BF16),
                pltpu.VMEM((size, cases), F32),
                pltpu.VMEM((size, cases), BF16),
                pltpu.VMEM((size, cases), BF16),
                pltpu.VMEM((size, cases), F32),
                pltpu.VMEM((count, 1, lanes), F32),
                pltpu.VMEM((subs * height, width), BF16),
                pltpu.VMEM((cols * blocks, width), F32),
                pltpu.VMEM((cols, blocks, width), BF16),
                pltpu.VMEM((cols, blocks, width), BF16),
                pltpu.VMEM((count // group, blocks, group * primals), BF16),
                pltpu.VMEM((count, primals, cases), BF16),
                pltpu.VMEM((count, 2, cases), F32),
                pltpu.SemaphoreType.DMA((8,)),
                pltpu.SemaphoreType.DMA((4,)),
                pltpu.SemaphoreType.DMA((4,)),
                pltpu.SemaphoreType.DMA((4,)),
                pltpu.SemaphoreType.DMA((4,)),
                pltpu.SemaphoreType.DMA((4,)),
                pltpu.SemaphoreType.DMA((4,)),
                pltpu.SemaphoreType.DMA((5,)),
                pltpu.SemaphoreType.DMA((5,)),
                pltpu.SemaphoreType.REGULAR((4,)),
                pltpu.SemaphoreType.REGULAR((1,)),
            ],
            compiler_params=pltpu.CompilerParams(
                collective_id=0, has_side_effects=True, vmem_limit_bytes=limit
            ),
        )(*(pltpu.with_memory_space_constraint(x, pltpu.HBM) for x in (rhs, schur, local_inverse, basis, coarse_inverse, primal_index, neighbour_dof)))
        return (alpha * first).astype(BF16)[None]

    return jax.shard_map(
        step,
        mesh=mesh,
        in_specs=(
            P(("sub", "col"), None, None),
            P(("sub", "col"), None, None),
            P(("sub", "col"), None, None),
            P(("sub", "col"), None, None),
            P("sub", "col"),
            P(("sub", "col"), None),
            P(("sub", "col"), None),
        ),
        out_specs=P(("sub", "col"), None, None),
        check_vma=False,
    )
```

```python
import functools
import math

import jax
import jax.numpy as jnp
from jax import lax
from jax.experimental import pallas as pl
from jax.experimental.pallas import tpu as pltpu
from jax.sharding import PartitionSpec as P

MESH = pl.DeviceIdType.MESH
F32 = jnp.float32
BF16 = jnp.bfloat16


def kernel(
    subs, cols,
    rhs_hbm, schur_hbm, inverse_hbm, basis_hbm, coarse_hbm, index_hbm, links_hbm,
    first_ref, alpha_ref,
    basis_ref, index_ref, links_ref, rhs_ref, schur_ref, inverse_ref,
    picks, halo_rhs, halo_z, halo_basis, lift, lift_image, z_ref, z_half, image_ref,
    indices, slab, picked, chosen, arrived, columns, loads, sums,
    local_sem, halo_send, halo_recv, z_send, z_recv, basis_send, basis_recv, all_send, all_recv,
    face_ack, all_ack,
):
    count = subs * cols
    row = lax.axis_index("sub")
    column = lax.axis_index("col")
    me = row * cols + column
    size = rhs_ref.shape[0]
    face = size // 4
    primals = index_ref.shape[1]
    height, width = coarse_hbm.shape
    cases = rhs_ref.shape[1]
    blocks = 5 * primals
    group = math.gcd(count, 32)
    straight = count <= 64

    def place(target):
        return (target // cols, target % cols)

    def span(f):
        return pl.ds(pl.multiple_of(f * face, face), face)

    half_way = (row * 2) // subs

    def each_other(act):
        def body(step, carry):
            q = step // cols
            high, low = subs - 1 - q, q
            high = high - (row - high + subs) // subs
            low = low + (low - row + subs) // subs
            target_row = (1 - half_way) * high + half_way * low
            act((target_row, (column + step) % cols))
            return carry

        lax.fori_loop(0, (subs - 1) * cols, body, 0, unroll=straight)
        for step in range(1, cols):
            act((row, (column + step) % cols))

    def loop(start, stop, act):
        def body(target, carry):
            act(target)
            return carry

        lax.fori_loop(start, stop, body, 0)

    barrier = pltpu.get_barrier_semaphore()

    def signal(semaphore, target):
        pl.semaphore_signal(semaphore, inc=1, device_id=target, device_id_type=MESH)

    loop(0, subs - 1 - row, lambda q: signal(barrier, (subs - 1 - q, column)))
    loop(column + 1, cols, lambda k: signal(barrier, (row, k)))

    small_loads = [
        pltpu.make_async_copy(source, target, local_sem.at[4 + number])
        for number, (source, target) in enumerate(
            ((links_hbm, links_ref), (index_hbm, index_ref), (basis_hbm, basis_ref),
             (coarse_hbm, slab.at[pl.ds(row * height, height)]))
        )
    ]
    for load in small_loads:
        load.start()
    load_rhs = pltpu.make_async_copy(rhs_hbm.at[0], rhs_ref, local_sem.at[0])
    load_inverse = pltpu.make_async_copy(inverse_hbm.at[0], inverse_ref, local_sem.at[1])
    load_schur = pltpu.make_async_copy(schur_hbm.at[0], schur_ref, local_sem.at[2])
    load_rhs.start()
    load_inverse.start()
    load_schur.start()

    def facing(g):
        return 1 - g if g < 2 else 5 - g

    def partner(g):
        if g < 2:
            return ((row + subs + 2 * g - 1) % subs, column)
        return (row, (column + cols + 2 * g - 5) % cols)

    def exchange(source, target, send, recv, g):
        return pltpu.make_async_remote_copy(
            src_ref=source, dst_ref=target.at[facing(g)], send_sem=send.at[g], recv_sem=recv.at[facing(g)],
            device_id=partner(g), device_id_type=MESH,
        )

    rhs_copies = [
        exchange(rhs_hbm.at[0, pl.ds(g * face, face)], halo_rhs, halo_send, halo_recv, g) for g in range(4)
    ]
    basis_copies = [
        exchange(basis_hbm.at[0, :, pl.ds(g * face, face)], halo_basis, basis_send, basis_recv, g)
        for g in range(4)
    ]
    z_copies = [
        exchange(z_half.at[pl.ds(g * face, face)], halo_z, z_send, z_recv, g) for g in range(4)
    ]

    def row_z_copy(g):
        return pltpu.make_async_remote_copy(
            src_ref=z_half.at[span(g)], dst_ref=halo_z.at[1 - g], send_sem=z_send.at[g], recv_sem=z_recv.at[1 - g],
            device_id=((row + subs + 2 * g - 1) % subs, column), device_id_type=MESH,
        )

    lower = (row > 0, row == subs - 1, column > 0, column == cols - 1)
    higher = (row == 0, row < subs - 1, column == 0, column < cols - 1)

    @pl.when(me > 0)
    def _():
        pl.semaphore_wait(barrier, row + column)

    for g in (1, 0, 2, 3):
        @pl.when(lower[g])
        def _(g=g):
            signal(face_ack.at[facing(g)], partner(g))
            rhs_copies[g].start()
            basis_copies[g].start()

    loop(0, row, lambda target: signal(all_ack.at[0], (target, column)))
    loop(0, column, lambda target: signal(all_ack.at[0], (row, target)))

    def send_coarse(target):
        pltpu.make_async_remote_copy(
            src_ref=coarse_hbm,
            dst_ref=slab.at[pl.ds(row * height, height)],
            send_sem=all_send.at[4],
            recv_sem=all_recv.at[4],
            device_id=(target, column),
            device_id_type=MESH,
        ).start()

    def send_slot(slots, number):
        return lambda target: pltpu.make_async_remote_copy(
            src_ref=slots.at[me],
            dst_ref=slots.at[me],
            send_sem=all_send.at[number],
            recv_sem=all_recv.at[number],
            device_id=target,
            device_id_type=MESH,
        ).start()

    loop(0, row, send_coarse)
    for load in small_loads:
        load.wait()
    lanes = indices.shape[2]
    indices[me] = jnp.zeros((1, lanes), F32)
    indices[me, :, pl.ds(0, primals)] = index_ref[...].astype(F32)

    offsets = (face, 0, 3 * face, 2 * face)
    for f in range(4):
        places = links_ref[:, f * face : (f + 1) * face] - offsets[f]
        hit = lax.broadcasted_iota(jnp.int32, (face, face), 0) == places
        picks[f] = jnp.where(hit, 1.0, 0.0).astype(F32).T.astype(BF16)

    for g in (3, 2, 1, 0):
        @pl.when(higher[g])
        def _(g=g):
            pl.semaphore_wait(face_ack.at[g], 1)
            rhs_copies[g].start()
            basis_copies[g].start()

    @pl.when(me < count - 1)
    def _():
        pl.semaphore_wait(all_ack.at[0], subs + cols - 2 - row - column)

    for step in range(1, cols):
        signal(all_ack.at[1], (row, (column + step) % cols))
    loop(0, subs - 1 - row, lambda q: send_coarse(subs - 1 - q))
    pl.semaphore_wait(all_ack.at[1], cols - 1)
    each_other(send_slot(indices, 0))

    def wait_face(target, recv, f):
        pltpu.make_async_copy(target.at[f], target.at[f], recv.at[f]).wait()

    def wait_part(part, sems, number):
        pltpu.make_async_copy(part, part, sems.at[number]).wait()

    others = pl.ds(0, count - 1)

    last = (row + 1) // subs
    load_rhs.wait()
    load = jnp.zeros((primals, cases), F32)
    load_inverse.wait()
    for number, f in enumerate((2, 3, 1 - last, last)):
        block = span(f)
        wait_face(halo_rhs, halo_recv, f)
        got = jnp.dot(picks[f], halo_rhs[f], preferred_element_type=F32)
        residual = rhs_ref[block, :].astype(F32) + got
        first_ref[block, :] = residual
        part = (residual * 0.5).astype(BF16)
        load += jnp.dot(basis_ref[0, :, block], part, preferred_element_type=F32)
        if number == 0:
            for h in range(4):
                rows = span(h)
                z_ref[rows, :] = jnp.dot(inverse_ref[rows, block], part, preferred_element_type=F32)
        elif number < 3:
            for h in range(4):
                rows = span(h)
                z_ref[rows, :] += jnp.dot(inverse_ref[rows, block], part, preferred_element_type=F32)
        else:
            for turn, h in enumerate((last, 1 - last, 2, 3)):
                rows = span(h)
                value = z_ref[rows, :] + jnp.dot(inverse_ref[rows, block], part, preferred_element_type=F32)
                value = value * 0.5
                z_ref[rows, :] = value
                z_half[rows, :] = value.astype(BF16)
                (row_z_copy(h) if turn < 2 else z_copies[h]).start()
                if turn == 0:
                    loads[me] = load.astype(BF16)
                    each_other(send_slot(loads, 1))
    begun = jnp.sum(first_ref[...] * z_ref[...], axis=0, keepdims=True)

    def spread(start, extent, number):
        values = indices[pl.ds(start, number)]
        values = jnp.broadcast_to(values, (number, primals, lanes))
        diagonal = lax.broadcasted_iota(jnp.int32, values.shape, 1) == lax.broadcasted_iota(
            jnp.int32, values.shape, 2
        )
        named = jnp.sum(jnp.where(diagonal, values, 0.0), axis=2, keepdims=True)
        named = named.astype(jnp.int32)
        return jnp.broadcast_to(named, (number, primals, extent))

    wait_part(indices.at[others], all_recv, 0)
    total_rows = subs * height
    chunk = math.gcd(total_rows, 256)
    own = spread(row * cols, chunk, cols)
    up = spread((row + subs - 1) % subs * cols, chunk, cols)
    down = spread((row + 1) % subs * cols, chunk, cols)
    named = jnp.concatenate(
        [
            source[k : k + 1]
            for j in range(cols)
            for source, k in ((own, j), (up, j), (down, j), (own, (j + cols - 1) % cols), (own, (j + 1) % cols))
        ],
        axis=0,
    )
    wait_part(slab.at[pl.ds(0, (subs - 1) * height)], all_recv, 4)

    def choose(k, carry):
        hit = lax.broadcasted_iota(jnp.int32, named.shape, 2) == named - k * chunk
        hit = jnp.where(hit, 1.0, 0.0).astype(F32).reshape(cols * blocks, chunk).astype(BF16)
        part = slab[pl.ds(pl.multiple_of(k * chunk, chunk), chunk), :]
        picked[...] += jnp.dot(hit, part, preferred_element_type=F32)
        return carry

    picked[...] = jnp.zeros_like(picked)
    lax.fori_loop(0, total_rows // chunk, choose, 0)
    chosen[...] = picked[...].reshape(cols, blocks, width).astype(BF16)
    arrived[column] = chosen[column]
    for step in range(1, cols):
        target = (column + step) % cols
        pltpu.make_async_remote_copy(
            src_ref=chosen.at[target],
            dst_ref=arrived.at[column],
            send_sem=all_send.at[3],
            recv_sem=all_recv.at[3],
            device_id=(row, target),
            device_id_type=MESH,
        ).start()

    for f in range(4):
        wait_face(halo_basis, basis_recv, f)
        mine = basis_ref[0, :, f * face : (f + 1) * face].astype(F32) * 0.5
        theirs = halo_basis[f].astype(F32) * 0.5
        none = jnp.zeros_like(theirs)
        both = jnp.concatenate([none] * (f + 1) + [theirs] + [none] * (3 - f), axis=0).astype(BF16)
        turned = lax.dot_general(picks[f], both, (((1,), (1,)), ((), ())), preferred_element_type=F32)
        kept = jnp.concatenate([mine] + [none] * 4, axis=0).T
        lift[f * face : (f + 1) * face, :] = (turned + kept).astype(BF16)

    load_schur.wait()
    for h in range(4):
        rows = pl.ds(h * face, face)
        lift_image[rows, :] = jnp.dot(
            schur_ref[rows, :], lift[...], preferred_element_type=F32
        ).astype(BF16)

    wait_part(arrived.at[pl.ds(0, cols - 1)], all_recv, 3)

    def arrange(g, carry):
        total = jnp.zeros((blocks, group * primals), F32)
        for j in range(cols):
            named = spread(g * group, width, group) - j * width
            hit = lax.broadcasted_iota(jnp.int32, named.shape, 2) == named
            hit = jnp.where(hit, 1.0, 0.0).astype(F32).reshape(group * primals, width).astype(BF16)
            total += lax.dot_general(
                arrived[j], hit, (((1,), (1,)), ((), ())), preferred_element_type=F32
            )
        columns[g] = total.astype(BF16)
        return carry

    lax.fori_loop(0, count // group, arrange, 0)

    for number, f in enumerate((2, 3, 1 - last, last)):
        block = span(f)
        wait_face(halo_z, z_recv, f)
        value = z_ref[block, :] + jnp.dot(picks[f], halo_z[f], preferred_element_type=F32)
        first_ref[block, :] = value
        part = value.astype(BF16)
        for h in range(4):
            rows = pl.ds(h * face, face)
            image = jnp.dot(schur_ref[rows, block], part, preferred_element_type=F32)
            if number == 0:
                image_ref[rows, :] = image
            else:
                image_ref[rows, :] += image

    wait_part(loads.at[others], all_recv, 1)

    def solve(g, total):
        part = loads[pl.ds(g * group, group)].astype(F32).reshape(group * primals, cases)
        return total + jnp.dot(columns[g], part.astype(BF16), preferred_element_type=F32)

    taken = lax.fori_loop(0, count // group, solve, jnp.zeros((blocks, cases), F32))
    taken = taken.astype(BF16)
    ended = jnp.sum(load * taken[:primals].astype(F32), axis=0, keepdims=True)
    sums[me, pl.ds(0, 1), :] = begun + ended

    total = jnp.zeros((1, cases), F32)
    for h in range(4):
        rows = pl.ds(h * face, face)
        value = first_ref[rows, :] + jnp.dot(lift[rows, :], taken, preferred_element_type=F32)
        image = image_ref[rows, :] + jnp.dot(lift_image[rows, :], taken, preferred_element_type=F32)
        first_ref[rows, :] = value
        total += jnp.sum(value * image, axis=0, keepdims=True)
    sums[me, pl.ds(1, 1), :] = total
    each_other(send_slot(sums, 2))
    for copy in rhs_copies + basis_copies + z_copies:
        copy.wait_send()
    wait_part(indices.at[others], all_send, 0)
    wait_part(loads.at[others], all_send, 1)
    wait_part(arrived.at[pl.ds(0, cols - 1)], all_send, 3)
    wait_part(slab.at[pl.ds(0, (subs - 1) * height)], all_send, 4)
    wait_part(sums.at[others], all_recv, 2)
    whole = jnp.sum(sums[...], axis=0)
    alpha_ref[...] = whole[0:1, :] / whole[1:2, :]
    wait_part(sums.at[others], all_send, 2)


def solution(mesh):
    subs, cols = mesh.shape["sub"], mesh.shape["col"]
    count = subs * cols

    def step(rhs, schur, local_inverse, basis, coarse_inverse, primal_index, neighbour_dof):
        size, cases = rhs.shape[1:]
        face = size // 4
        primals = primal_index.shape[1]
        height, width = coarse_inverse.shape
        lanes = 128 * pl.cdiv(primals, 128)
        wide = 128 * pl.cdiv(width, 128)
        blocks = 5 * primals
        group = math.gcd(count, 32)
        anywhere = pl.BlockSpec(memory_space=pltpu.HBM)
        near = pl.BlockSpec(memory_space=pltpu.VMEM)
        fixed = 4 * size * size + 8 * face * face + 24 * size * cases + 8 * 128 * size
        slots = count * (4 * 8 * lanes + 2 * primals * cases * 2 + 4 * 8 * cases)
        coarse = 2 * subs * height * wide + 12 * cols * blocks * wide + 4 * count * primals * blocks
        limit = min(fixed + slots + coarse + 6 * 1024 * 1024, 63 * 1024 * 1024)
        first, alpha = pl.pallas_call(
            functools.partial(kernel, subs, cols),
            out_shape=(
                jax.ShapeDtypeStruct((size, cases), F32),
                jax.ShapeDtypeStruct((1, cases), F32),
            ),
            in_specs=[anywhere] * 7,
            out_specs=(near, near),
            scratch_shapes=[
                pltpu.VMEM(basis.shape, BF16),
                pltpu.VMEM(primal_index.shape, jnp.int32),
                pltpu.VMEM(neighbour_dof.shape, jnp.int32),
                pltpu.VMEM((size, cases), BF16),
                pltpu.VMEM((size, size), BF16),
                pltpu.VMEM((size, size), BF16),
                pltpu.VMEM((4, face, face), BF16),
                pltpu.VMEM((4, face, cases), BF16),
                pltpu.VMEM((4, face, cases), BF16),
                pltpu.VMEM((4, primals, face), BF16),
                pltpu.VMEM((size, blocks), BF16),
                pltpu.VMEM((size, blocks), BF16),
                pltpu.VMEM((size, cases), F32),
                pltpu.VMEM((size, cases), BF16),
                pltpu.VMEM((size, cases), F32),
                pltpu.VMEM((count, 1, lanes), F32),
                pltpu.VMEM((subs * height, width), BF16),
                pltpu.VMEM((cols * blocks, width), F32),
                pltpu.VMEM((cols, blocks, width), BF16),
                pltpu.VMEM((cols, blocks, width), BF16),
                pltpu.VMEM((count // group, blocks, group * primals), BF16),
                pltpu.VMEM((count, primals, cases), BF16),
                pltpu.VMEM((count, 2, cases), F32),
                pltpu.SemaphoreType.DMA((8,)),
                pltpu.SemaphoreType.DMA((4,)),
                pltpu.SemaphoreType.DMA((4,)),
                pltpu.SemaphoreType.DMA((4,)),
                pltpu.SemaphoreType.DMA((4,)),
                pltpu.SemaphoreType.DMA((4,)),
                pltpu.SemaphoreType.DMA((4,)),
                pltpu.SemaphoreType.DMA((5,)),
                pltpu.SemaphoreType.DMA((5,)),
                pltpu.SemaphoreType.REGULAR((4,)),
                pltpu.SemaphoreType.REGULAR((2,)),
            ],
            compiler_params=pltpu.CompilerParams(
                collective_id=0, has_side_effects=True, vmem_limit_bytes=limit
            ),
        )(*(pltpu.with_memory_space_constraint(x, pltpu.HBM) for x in (rhs, schur, local_inverse, basis, coarse_inverse, primal_index, neighbour_dof)))
        return (alpha * first).astype(BF16)[None]

    return jax.shard_map(
        step,
        mesh=mesh,
        in_specs=(
            P(("sub", "col"), None, None),
            P(("sub", "col"), None, None),
            P(("sub", "col"), None, None),
            P(("sub", "col"), None, None),
            P("sub", "col"),
            P(("sub", "col"), None),
            P(("sub", "col"), None),
        ),
        out_specs=P(("sub", "col"), None, None),
        check_vma=False,
    )
```

```python
import functools
import math

import jax
import jax.numpy as jnp
from jax import lax
from jax.experimental import pallas as pl
from jax.experimental.pallas import tpu as pltpu
from jax.sharding import PartitionSpec as P

MESH = pl.DeviceIdType.MESH
F32 = jnp.float32
BF16 = jnp.bfloat16
PIECES = 4


def kernel(
    subs, cols,
    rhs_hbm, schur_hbm, inverse_hbm, basis_hbm, coarse_hbm, index_hbm, links_hbm,
    first_ref, alpha_ref,
    basis_ref, index_ref, links_ref, rhs_ref, schur_ref, inverse_ref,
    picks, halo_rhs, halo_z, halo_basis, lift, lift_image, z_ref, z_half, image_ref,
    indices, slab, picked, chosen, arrived, columns, loads, sums,
    local_sem, halo_send, halo_recv, z_send, z_recv, basis_send, basis_recv, all_send, all_recv,
    face_ack, all_ack,
):
    count = subs * cols
    row = lax.axis_index("sub")
    column = lax.axis_index("col")
    me = row * cols + column
    size = rhs_ref.shape[0]
    face = size // 4
    primals = index_ref.shape[1]
    height, width = coarse_hbm.shape
    cases = rhs_ref.shape[1]
    blocks = 5 * primals
    group = math.gcd(count, 32)
    straight = count <= 64

    def place(target):
        return (target // cols, target % cols)

    def span(f):
        return pl.ds(pl.multiple_of(f * face, face), face)

    half_way = (row * 2) // subs

    def each_other(act):
        def body(step, carry):
            q = step // cols
            high, low = subs - 1 - q, q
            high = high - (row - high + subs) // subs
            low = low + (low - row + subs) // subs
            target_row = (1 - half_way) * high + half_way * low
            act((target_row, (column + step) % cols))
            return carry

        lax.fori_loop(0, (subs - 1) * cols, body, 0, unroll=straight)
        for step in range(1, cols):
            act((row, (column + step) % cols))

    def loop(start, stop, act):
        def body(target, carry):
            act(target)
            return carry

        lax.fori_loop(start, stop, body, 0)

    barrier = pltpu.get_barrier_semaphore()

    def signal(semaphore, target):
        pl.semaphore_signal(semaphore, inc=1, device_id=target, device_id_type=MESH)

    loop(0, subs - 1 - row, lambda q: signal(barrier, (subs - 1 - q, column)))
    loop(column + 1, cols, lambda k: signal(barrier, (row, k)))

    small_loads = [
        pltpu.make_async_copy(source, target, local_sem.at[4 + number])
        for number, (source, target) in enumerate(
            ((links_hbm, links_ref), (index_hbm, index_ref), (basis_hbm, basis_ref),
             (coarse_hbm, slab.at[pl.ds(row * height, height)]))
        )
    ]
    for load in small_loads:
        load.start()
    load_rhs = pltpu.make_async_copy(rhs_hbm.at[0], rhs_ref, local_sem.at[0])
    load_inverse = pltpu.make_async_copy(inverse_hbm.at[0], inverse_ref, local_sem.at[1])
    load_schur = pltpu.make_async_copy(schur_hbm.at[0], schur_ref, local_sem.at[2])
    load_rhs.start()
    load_inverse.start()
    load_schur.start()

    def facing(g):
        return 1 - g if g < 2 else 5 - g

    def partner(g):
        if g < 2:
            return ((row + subs + 2 * g - 1) % subs, column)
        return (row, (column + cols + 2 * g - 5) % cols)

    def exchange(source, target, send, recv, g):
        return pltpu.make_async_remote_copy(
            src_ref=source, dst_ref=target.at[facing(g)], send_sem=send.at[g], recv_sem=recv.at[facing(g)],
            device_id=partner(g), device_id_type=MESH,
        )

    rhs_copies = [
        exchange(rhs_hbm.at[0, pl.ds(g * face, face)], halo_rhs, halo_send, halo_recv, g) for g in range(4)
    ]
    basis_copies = [
        exchange(basis_hbm.at[0, :, pl.ds(g * face, face)], halo_basis, basis_send, basis_recv, g)
        for g in range(4)
    ]
    z_copies = [
        exchange(z_half.at[pl.ds(g * face, face)], halo_z, z_send, z_recv, g) for g in range(4)
    ]

    def row_z_copy(g):
        return pltpu.make_async_remote_copy(
            src_ref=z_half.at[span(g)], dst_ref=halo_z.at[1 - g], send_sem=z_send.at[g], recv_sem=z_recv.at[1 - g],
            device_id=((row + subs + 2 * g - 1) % subs, column), device_id_type=MESH,
        )

    lower = (row > 0, row == subs - 1, column > 0, column == cols - 1)
    higher = (row == 0, row < subs - 1, column == 0, column < cols - 1)

    @pl.when(me > 0)
    def _():
        pl.semaphore_wait(barrier, row + column)

    for g in (1, 0, 2, 3):
        @pl.when(lower[g])
        def _(g=g):
            signal(face_ack.at[facing(g)], partner(g))
            rhs_copies[g].start()
            basis_copies[g].start()

    loop(0, row, lambda target: signal(all_ack.at[0], (target, column)))
    loop(0, column, lambda target: signal(all_ack.at[0], (row, target)))

    def send_coarse(target):
        pltpu.make_async_remote_copy(
            src_ref=coarse_hbm,
            dst_ref=slab.at[pl.ds(row * height, height)],
            send_sem=all_send.at[4],
            recv_sem=all_recv.at[4],
            device_id=(target, column),
            device_id_type=MESH,
        ).start()

    def send_slot(slots, number):
        return lambda target: pltpu.make_async_remote_copy(
            src_ref=slots.at[me],
            dst_ref=slots.at[me],
            send_sem=all_send.at[number],
            recv_sem=all_recv.at[number],
            device_id=target,
            device_id_type=MESH,
        ).start()

    loop(0, row, send_coarse)
    for load in small_loads:
        load.wait()
    lanes = indices.shape[2]
    indices[me] = jnp.zeros((1, lanes), F32)
    indices[me, :, pl.ds(0, primals)] = index_ref[...].astype(F32)

    offsets = (face, 0, 3 * face, 2 * face)
    for f in range(4):
        places = links_ref[:, f * face : (f + 1) * face] - offsets[f]
        hit = lax.broadcasted_iota(jnp.int32, (face, face), 0) == places
        picks[f] = jnp.where(hit, 1.0, 0.0).astype(F32).T.astype(BF16)

    for g in (3, 2, 1, 0):
        @pl.when(higher[g])
        def _(g=g):
            pl.semaphore_wait(face_ack.at[g], 1)
            rhs_copies[g].start()
            basis_copies[g].start()

    @pl.when(me < count - 1)
    def _():
        pl.semaphore_wait(all_ack.at[0], subs + cols - 2 - row - column)

    for step in range(1, cols):
        signal(all_ack.at[1], (row, (column + step) % cols))
    loop(0, subs - 1 - row, lambda q: send_coarse(subs - 1 - q))
    pl.semaphore_wait(all_ack.at[1], cols - 1)
    each_other(send_slot(indices, 0))

    def wait_face(target, recv, f):
        pltpu.make_async_copy(target.at[f], target.at[f], recv.at[f]).wait()

    def wait_part(part, sems, number):
        pltpu.make_async_copy(part, part, sems.at[number]).wait()

    others = pl.ds(0, count - 1)

    last = (row + 1) // subs
    load_rhs.wait()
    load_inverse.wait()

    def settle(f):
        block = span(f)
        wait_face(halo_rhs, halo_recv, f)
        got = jnp.dot(picks[f], halo_rhs[f], preferred_element_type=F32)
        residual = rhs_ref[block, :].astype(F32) + got
        first_ref[block, :] = residual
        part = (residual * 0.5).astype(BF16)
        return part, jnp.dot(basis_ref[0, :, block], part, preferred_element_type=F32)

    part, load = settle(2)
    other, more = settle(3)
    load += more
    part = jnp.concatenate([part, other], axis=0)
    for h in range(PIECES):
        rows = pl.ds(h * (size // PIECES), size // PIECES)
        z_ref[rows, :] = jnp.dot(inverse_ref[rows, 2 * face :], part, preferred_element_type=F32)
    part, more = settle(1 - last)
    load += more
    for h in range(PIECES):
        rows = pl.ds(h * (size // PIECES), size // PIECES)
        z_ref[rows, :] += jnp.dot(inverse_ref[rows, span(1 - last)], part, preferred_element_type=F32)
    part, more = settle(last)
    load += more
    for turn, h in enumerate((last, 1 - last, 2, 3)):
        rows = span(h)
        value = z_ref[rows, :] + jnp.dot(inverse_ref[rows, span(last)], part, preferred_element_type=F32)
        value = value * 0.5
        z_ref[rows, :] = value
        z_half[rows, :] = value.astype(BF16)
        (row_z_copy(h) if turn < 2 else z_copies[h]).start()
        if turn == 0:
            loads[me] = load.astype(BF16)
            each_other(send_slot(loads, 1))
    begun = jnp.sum(first_ref[...] * z_ref[...], axis=0, keepdims=True)

    def spread(start, extent, number):
        values = indices[pl.ds(start, number)]
        values = jnp.broadcast_to(values, (number, primals, lanes))
        diagonal = lax.broadcasted_iota(jnp.int32, values.shape, 1) == lax.broadcasted_iota(
            jnp.int32, values.shape, 2
        )
        named = jnp.sum(jnp.where(diagonal, values, 0.0), axis=2, keepdims=True)
        named = named.astype(jnp.int32)
        return jnp.broadcast_to(named, (number, primals, extent))

    wait_part(indices.at[others], all_recv, 0)
    total_rows = subs * height
    chunk = math.gcd(total_rows, 256)
    own = spread(row * cols, chunk, cols)
    up = spread((row + subs - 1) % subs * cols, chunk, cols)
    down = spread((row + 1) % subs * cols, chunk, cols)
    named = jnp.concatenate(
        [
            source[k : k + 1]
            for j in range(cols)
            for source, k in ((own, j), (up, j), (down, j), (own, (j + cols - 1) % cols), (own, (j + 1) % cols))
        ],
        axis=0,
    )
    wait_part(slab.at[pl.ds(0, (subs - 1) * height)], all_recv, 4)

    def choose(k, carry):
        hit = lax.broadcasted_iota(jnp.int32, named.shape, 2) == named - k * chunk
        hit = jnp.where(hit, 1.0, 0.0).astype(F32).reshape(cols * blocks, chunk).astype(BF16)
        part = slab[pl.ds(pl.multiple_of(k * chunk, chunk), chunk), :]
        picked[...] += jnp.dot(hit, part, preferred_element_type=F32)
        return carry

    picked[...] = jnp.zeros_like(picked)
    lax.fori_loop(0, total_rows // chunk, choose, 0)
    chosen[...] = picked[...].reshape(cols, blocks, width).astype(BF16)
    arrived[column] = chosen[column]
    for step in range(1, cols):
        target = (column + step) % cols
        pltpu.make_async_remote_copy(
            src_ref=chosen.at[target],
            dst_ref=arrived.at[column],
            send_sem=all_send.at[3],
            recv_sem=all_recv.at[3],
            device_id=(row, target),
            device_id_type=MESH,
        ).start()

    for f in range(4):
        wait_face(halo_basis, basis_recv, f)
        mine = basis_ref[0, :, f * face : (f + 1) * face].astype(F32) * 0.5
        theirs = halo_basis[f].astype(F32) * 0.5
        none = jnp.zeros_like(theirs)
        both = jnp.concatenate([none] * (f + 1) + [theirs] + [none] * (3 - f), axis=0).astype(BF16)
        turned = lax.dot_general(picks[f], both, (((1,), (1,)), ((), ())), preferred_element_type=F32)
        kept = jnp.concatenate([mine] + [none] * 4, axis=0).T
        lift[f * face : (f + 1) * face, :] = (turned + kept).astype(BF16)

    load_schur.wait()
    for h in range(4):
        rows = pl.ds(h * face, face)
        lift_image[rows, :] = jnp.dot(
            schur_ref[rows, :], lift[...], preferred_element_type=F32
        ).astype(BF16)

    def meet(faces, fresh):
        parts = []
        for f in faces:
            block = span(f)
            wait_face(halo_z, z_recv, f)
            value = z_ref[block, :] + jnp.dot(picks[f], halo_z[f], preferred_element_type=F32)
            first_ref[block, :] = value
            parts.append(value.astype(BF16))
        part = parts[0] if len(parts) == 1 else jnp.concatenate(parts, axis=0)
        wide = pl.ds(pl.multiple_of(faces[0] * face, face), len(faces) * face)
        for h in range(PIECES):
            rows = pl.ds(h * (size // PIECES), size // PIECES)
            image = jnp.dot(schur_ref[rows, wide], part, preferred_element_type=F32)
            if fresh:
                image_ref[rows, :] = image
            else:
                image_ref[rows, :] += image

    meet((2, 3), True)
    meet((1 - last,), False)

    wait_part(arrived.at[pl.ds(0, cols - 1)], all_recv, 3)

    def arrange(g, carry):
        total = jnp.zeros((blocks, group * primals), F32)
        for j in range(cols):
            named = spread(g * group, width, group) - j * width
            hit = lax.broadcasted_iota(jnp.int32, named.shape, 2) == named
            hit = jnp.where(hit, 1.0, 0.0).astype(F32).reshape(group * primals, width).astype(BF16)
            total += lax.dot_general(
                arrived[j], hit, (((1,), (1,)), ((), ())), preferred_element_type=F32
            )
        columns[g] = total.astype(BF16)
        return carry

    lax.fori_loop(0, count // group, arrange, 0)

    meet((last,), False)

    wait_part(loads.at[others], all_recv, 1)

    def solve(g, total):
        part = loads[pl.ds(g * group, group)].astype(F32).reshape(group * primals, cases)
        return total + jnp.dot(columns[g], part.astype(BF16), preferred_element_type=F32)

    taken = lax.fori_loop(0, count // group, solve, jnp.zeros((blocks, cases), F32))
    taken = taken.astype(BF16)
    ended = jnp.sum(load * taken[:primals].astype(F32), axis=0, keepdims=True)
    sums[me, pl.ds(0, 1), :] = begun + ended

    total = jnp.zeros((1, cases), F32)
    for h in range(4):
        rows = pl.ds(h * face, face)
        value = first_ref[rows, :] + jnp.dot(lift[rows, :], taken, preferred_element_type=F32)
        image = image_ref[rows, :] + jnp.dot(lift_image[rows, :], taken, preferred_element_type=F32)
        first_ref[rows, :] = value
        total += jnp.sum(value * image, axis=0, keepdims=True)
    sums[me, pl.ds(1, 1), :] = total
    each_other(send_slot(sums, 2))
    for copy in rhs_copies + basis_copies + z_copies:
        copy.wait_send()
    wait_part(indices.at[others], all_send, 0)
    wait_part(loads.at[others], all_send, 1)
    wait_part(arrived.at[pl.ds(0, cols - 1)], all_send, 3)
    wait_part(slab.at[pl.ds(0, (subs - 1) * height)], all_send, 4)
    wait_part(sums.at[others], all_recv, 2)
    whole = jnp.sum(sums[...], axis=0)
    alpha_ref[...] = whole[0:1, :] / whole[1:2, :]
    wait_part(sums.at[others], all_send, 2)


def solution(mesh):
    subs, cols = mesh.shape["sub"], mesh.shape["col"]
    count = subs * cols

    def step(rhs, schur, local_inverse, basis, coarse_inverse, primal_index, neighbour_dof):
        size, cases = rhs.shape[1:]
        face = size // 4
        primals = primal_index.shape[1]
        height, width = coarse_inverse.shape
        lanes = 128 * pl.cdiv(primals, 128)
        wide = 128 * pl.cdiv(width, 128)
        blocks = 5 * primals
        group = math.gcd(count, 32)
        anywhere = pl.BlockSpec(memory_space=pltpu.HBM)
        near = pl.BlockSpec(memory_space=pltpu.VMEM)
        fixed = 4 * size * size + 8 * face * face + 24 * size * cases + 8 * 128 * size
        slots = count * (4 * 8 * lanes + 2 * primals * cases * 2 + 4 * 8 * cases)
        coarse = 2 * subs * height * wide + 12 * cols * blocks * wide + 4 * count * primals * blocks
        limit = min(fixed + slots + coarse + 6 * 1024 * 1024, 63 * 1024 * 1024)
        first, alpha = pl.pallas_call(
            functools.partial(kernel, subs, cols),
            out_shape=(
                jax.ShapeDtypeStruct((size, cases), F32),
                jax.ShapeDtypeStruct((1, cases), F32),
            ),
            in_specs=[anywhere] * 7,
            out_specs=(near, near),
            scratch_shapes=[
                pltpu.VMEM(basis.shape, BF16),
                pltpu.VMEM(primal_index.shape, jnp.int32),
                pltpu.VMEM(neighbour_dof.shape, jnp.int32),
                pltpu.VMEM((size, cases), BF16),
                pltpu.VMEM((size, size), BF16),
                pltpu.VMEM((size, size), BF16),
                pltpu.VMEM((4, face, face), BF16),
                pltpu.VMEM((4, face, cases), BF16),
                pltpu.VMEM((4, face, cases), BF16),
                pltpu.VMEM((4, primals, face), BF16),
                pltpu.VMEM((size, blocks), BF16),
                pltpu.VMEM((size, blocks), BF16),
                pltpu.VMEM((size, cases), F32),
                pltpu.VMEM((size, cases), BF16),
                pltpu.VMEM((size, cases), F32),
                pltpu.VMEM((count, 1, lanes), F32),
                pltpu.VMEM((subs * height, width), BF16),
                pltpu.VMEM((cols * blocks, width), F32),
                pltpu.VMEM((cols, blocks, width), BF16),
                pltpu.VMEM((cols, blocks, width), BF16),
                pltpu.VMEM((count // group, blocks, group * primals), BF16),
                pltpu.VMEM((count, primals, cases), BF16),
                pltpu.VMEM((count, 2, cases), F32),
                pltpu.SemaphoreType.DMA((8,)),
                pltpu.SemaphoreType.DMA((4,)),
                pltpu.SemaphoreType.DMA((4,)),
                pltpu.SemaphoreType.DMA((4,)),
                pltpu.SemaphoreType.DMA((4,)),
                pltpu.SemaphoreType.DMA((4,)),
                pltpu.SemaphoreType.DMA((4,)),
                pltpu.SemaphoreType.DMA((5,)),
                pltpu.SemaphoreType.DMA((5,)),
                pltpu.SemaphoreType.REGULAR((4,)),
                pltpu.SemaphoreType.REGULAR((2,)),
            ],
            compiler_params=pltpu.CompilerParams(
                collective_id=0, has_side_effects=True, vmem_limit_bytes=limit
            ),
        )(*(pltpu.with_memory_space_constraint(x, pltpu.HBM) for x in (rhs, schur, local_inverse, basis, coarse_inverse, primal_index, neighbour_dof)))
        return (alpha * first).astype(BF16)[None]

    return jax.shard_map(
        step,
        mesh=mesh,
        in_specs=(
            P(("sub", "col"), None, None),
            P(("sub", "col"), None, None),
            P(("sub", "col"), None, None),
            P(("sub", "col"), None, None),
            P("sub", "col"),
            P(("sub", "col"), None),
            P(("sub", "col"), None),
        ),
        out_specs=P(("sub", "col"), None, None),
        check_vma=False,
    )
```
